32 devices in a mesh: ctx: 16 (over z, y, core), ch: 2 (over x).
Axes of the slice: x: 2, y: 2, z: 4, core: 2. Of those that a mesh axis runs over, the one named last changes fastest.
Arguments:
- inputs: float32 [12288, 2048], P('ctx', 'ch'), may hold values from -6 to 6
- cotangent: float32 [12288, 2048], P('ctx', 'ch'), may hold values from -6 to 6
- filter_rows: float32 [1536, 2048], P('ctx', 'ch'), may hold values from -0.15625 to 0.15625
- skip_gain: float32 [2048], P('ch'), may hold values from -1 to 1
- band_blocks: int32 [2048], P('ch'), may hold values from 1 to 2
Outputs:
- outputs: float32 [12288, 2048], P('ctx', 'ch')
- input_grad: float32 [2048, 12288], P(('ch', 'ctx'))
The draws below stay inside these ranges and needn't reach their ends.
All inputs are finite; a program needn't handle non-finite values.
Results may differ from the reference program's by a relative error of at most 0.00007.
Values sent between devices are 32-bit elements; how exact they have to be, the bound alone decides.
A program may use at most 192 MiB of HBM per device.

```python
import jax
import jax.numpy as jnp
from jax import lax

CH = 2048
BLK = 768
MAXB = 2
TOKENS = 12288
CH_DEV = 1024


def draw_band_blocks(key, part):
    groups = CH // CH_DEV
    key_cap, key_pick, key_each, key_slot = jax.random.split(key, 4)
    group_cap = jax.random.randint(key_cap, (groups,), 1, MAXB + 1)
    chosen = jax.random.randint(key_pick, (), 0, groups)
    group_ids = jnp.arange(groups, dtype=jnp.int32)
    group_cap = jnp.where(group_ids == chosen, MAXB, group_cap)
    raw_draw = jax.random.randint(key_each, (groups, CH_DEV), 0, MAXB * 8)
    band_vals = 1 + raw_draw % group_cap[:, None]
    slot_pos = jax.random.randint(key_slot, (), 0, CH_DEV)
    slot_ids = jnp.arange(CH_DEV, dtype=jnp.int32)
    in_chosen = group_ids[:, None] == chosen
    high_mask = in_chosen & (slot_ids[None, :] == slot_pos)
    low_mask = in_chosen & (slot_ids[None, :] == (slot_pos + 1) % CH_DEV)
    band_vals = jnp.where(high_mask, MAXB, jnp.where(low_mask, 1, band_vals))
    return band_vals.reshape(CH).astype(jnp.int32)


def block_levels(own_key, dims, pieces, low, high):
    def one(axis_at, parts):
        heights = jax.random.uniform(jax.random.fold_in(jax.random.fold_in(own_key, 6), axis_at), (parts,), jnp.float32, low / len(pieces), high / len(pieces))
        return jnp.repeat(jnp.exp(heights), dims[axis_at] // parts).reshape((-1,) + (1,) * (len(dims) - axis_at - 1))

    gain = one(*pieces[0])
    for cut in pieces[1:]:
        gain = gain * one(*cut)
    return gain


def noise(stream_key, extent, spread, limit, cuts=(), held_as=jnp.bfloat16):
    factor_of = block_levels(stream_key, extent, cuts, -0.22, 0.18) if cuts else 1.0
    result = jax.random.normal(stream_key, extent, jnp.float32) * spread * factor_of
    return jnp.minimum(jnp.maximum(result, -limit), limit).astype(held_as)


def setup_inputs(seed: int = 0) -> dict:
    arg_keys = jax.random.split(jax.random.key(seed), 6)
    return {
        "inputs": noise(arg_keys[0], (TOKENS, CH), 1.0, 6.0, ((0, 16), (1, 2)), jnp.float32),
        "cotangent": noise(arg_keys[1], (TOKENS, CH), 1.0, 6.0, ((0, 16), (1, 2)), jnp.float32),
        "filter_rows": noise(arg_keys[2], (MAXB * BLK, CH), (MAXB * BLK) ** -0.5, 0.15625, ((0, 16), (1, 2)), jnp.float32),
        "skip_gain": jnp.clip(jax.random.uniform(arg_keys[3], (CH,), jnp.float32, -1.0, 1.0) * block_levels(arg_keys[3], (CH,), ((0, 2),), -0.4, 0.0), -1.0, 1.0),
        "band_blocks": draw_band_blocks(jax.random.fold_in(arg_keys[5], 71), 0),
    }


def reference(inputs, cotangent, filter_rows, skip_gain, band_blocks):
    lag_index = jnp.arange(MAXB * BLK, dtype=jnp.int32)
    keep_mask = lag_index[:, None] < band_blocks[None, :] * BLK
    filter_full = jnp.where(keep_mask, filter_rows, jnp.zeros_like(filter_rows))
    length = 2 * TOKENS
    groups = CH // CH_DEV

    def per_group(packed):
        signal, grad_in, tap_rows, gain_row = packed
        spec_taps = jnp.fft.rfft(tap_rows, n=length, axis=0)
        spec_signal = jnp.fft.rfft(signal, n=length, axis=0)
        spec_grad = jnp.fft.rfft(grad_in, n=length, axis=0)
        forward_part = jnp.fft.irfft(spec_taps * spec_signal, n=length, axis=0)[:TOKENS]
        backward_part = jnp.fft.irfft(jnp.conj(spec_taps) * spec_grad, n=length, axis=0)[:TOKENS]
        forward_part = forward_part + gain_row[None, :] * signal
        backward_part = backward_part + gain_row[None, :] * grad_in
        return forward_part, backward_part.T

    stacked = (
        inputs.reshape(TOKENS, groups, CH_DEV).transpose(1, 0, 2),
        cotangent.reshape(TOKENS, groups, CH_DEV).transpose(1, 0, 2),
        filter_full.reshape(MAXB * BLK, groups, CH_DEV).transpose(1, 0, 2),
        skip_gain.reshape(groups, CH_DEV),
    )
    forward_all, backward_all = lax.map(per_group, stacked)
    outputs = forward_all.transpose(1, 0, 2).reshape(TOKENS, CH)
    input_grad = backward_all.reshape(CH, TOKENS)
    return outputs, input_grad
```

```python
import functools

import jax
import jax.numpy as jnp
import numpy as np
from jax import lax
from jax.experimental import pallas as pl
from jax.experimental.pallas import tpu as pltpu
from jax.sharding import PartitionSpec as P

SUB = 256
LEN = 2 * SUB
JCHUNK = 4


def stacked_halves(table):
    table = table.astype(np.float32)
    high = table.astype(jnp.bfloat16)
    low = (table - high.astype(np.float32)).astype(jnp.bfloat16)
    return np.concatenate([high, high, low], axis=0)


def transform_tables():
    time = np.arange(SUB)
    bins = np.arange(SUB)
    angle = 2.0 * np.pi * (time[:, None] * bins[None, :] % LEN) / LEN
    alternate = np.where(time % 2 == 0, 1.0, -1.0)
    real, imag = np.cos(angle), -np.sin(angle)
    imag[:, 0] = alternate
    forward = np.concatenate([real, imag], axis=1)
    back_real = 2.0 * np.cos(angle.T)
    back_real[0] = 1.0
    back_imag = -2.0 * np.sin(angle.T)
    back_imag[0] = alternate
    inverse = np.concatenate([back_real, back_imag], axis=0) / LEN
    return stacked_halves(forward), stacked_halves(inverse)


def precise_dot(value, table):
    high = value.astype(jnp.bfloat16)
    low = (value - high.astype(jnp.float32)).astype(jnp.bfloat16)
    return jnp.dot(
        jnp.concatenate([high, low, high], axis=1), table, preferred_element_type=jnp.float32
    )


def conv_kernel(adjoint, n, thirds, parts, x_ref, h_ref, d_ref, i_ref, o_ref, w_ref, s_ref, t_ref):
    group = h_ref.shape[0]
    halo = w_ref.shape[1] - n
    base = 0 if adjoint else halo
    lane = lax.broadcasted_iota(jnp.int32, (1, LEN), 1)
    sigma = jnp.where(lane % 2 == 0, 1.0, -1.0).astype(jnp.float32)
    first = lane[:, :SUB] == 0

    taps = jnp.concatenate([h_ref[:, p * SUB : (p + 1) * SUB] for p in range(parts)], axis=0)
    spec = precise_dot(taps, d_ref[...])
    real, imag = spec[:, :SUB], spec[:, SUB:]
    cross = jnp.where(first, 0.0, imag)
    t_ref[0] = real.reshape(parts, group, SUB)
    t_ref[1] = (-cross if adjoint else cross).reshape(parts, group, SUB)
    t_ref[2] = jnp.where(first, imag, real).reshape(parts, group, SUB)

    for t in range(thirds):
        rows = x_ref[:, :, t * SUB : (t + 1) * SUB].reshape(n * group, SUB)
        s_ref[t] = precise_dot(rows, d_ref[...]).reshape(n, group, LEN)

    pad_at = n if adjoint else 0
    w_ref[:, pad_at : pad_at + halo] = jnp.zeros((thirds, halo, group, LEN), jnp.float32)
    for t in range(thirds):
        if adjoint and t == thirds - 1:
            w_ref[t, n - 1] = s_ref[t, n - 1]
            w_ref[t, 0 : n - 1] = s_ref[t, 0 : n - 1] + sigma * s_ref[0, 1:n]
        elif adjoint:
            w_ref[t, 0:n] = s_ref[t] + sigma * s_ref[t + 1]
        elif t == 0:
            w_ref[0, base] = s_ref[0, 0]
            w_ref[0, base + 1 : base + n] = s_ref[0, 1:n] + sigma * s_ref[thirds - 1, 0 : n - 1]
        else:
            w_ref[t, base : base + n] = s_ref[t] + sigma * s_ref[t - 1]

    steps = n // JCHUNK

    def products(index, carry):
        rows = pl.ds(pl.multiple_of(index // steps * 8, 8), 8)
        start = index % steps * JCHUNK
        for t in range(thirds):
            acc_real = acc_imag = 0.0
            for p in range(parts):
                shift, third = divmod(t + p if adjoint else t - p, thirds)
                window = w_ref[third, pl.ds(start + base + shift, JCHUNK), rows, :]
                win_real, win_imag = window[..., :SUB], window[..., SUB:]
                tap_real, tap_cross, tap_last = (t_ref[i, p, rows, :] for i in range(3))
                acc_real += tap_real * win_real - tap_cross * win_imag
                acc_imag += tap_last * win_imag + tap_cross * win_real
            s_ref[t, pl.ds(start, JCHUNK), rows, :SUB] = acc_real
            s_ref[t, pl.ds(start, JCHUNK), rows, SUB:] = acc_imag
        return carry

    lax.fori_loop(0, steps * (group // 8), products, 0)

    for t in range(thirds):
        result = precise_dot(s_ref[t].reshape(n * group, LEN), i_ref[...])
        result = result.reshape(n, group, SUB)
        if adjoint:
            for j in range(n):
                at = (j * thirds + t) * SUB
                o_ref[:, at : at + SUB] = result[j]
        else:
            o_ref[:, :, t * SUB : (t + 1) * SUB] = result


def banded(signal, taps, tables, adjoint):
    n, channels, block = signal.shape
    thirds, parts = block // SUB, taps.shape[1] // SUB
    group = min(32, channels)
    halo = (thirds + parts - 2) // thirds
    if adjoint:
        out_shape = (channels, n * block)
        out_spec = pl.BlockSpec((group, n * block), lambda g: (g, 0))
    else:
        out_shape = (n, channels, block)
        out_spec = pl.BlockSpec((n, group, block), lambda g: (0, g, 0))
    whole = [pl.BlockSpec(table.shape, lambda g: (0, 0)) for table in tables]
    return pl.pallas_call(
        functools.partial(conv_kernel, adjoint, n, thirds, parts),
        out_shape=jax.ShapeDtypeStruct(out_shape, jnp.float32),
        grid=(channels // group,),
        in_specs=[
            pl.BlockSpec((n, group, block), lambda g: (0, g, 0)),
            pl.BlockSpec((group, taps.shape[1]), lambda g: (g, 0)),
            *whole,
        ],
        out_specs=out_spec,
        scratch_shapes=[
            pltpu.VMEM((thirds, n + halo, group, LEN), jnp.float32),
            pltpu.VMEM((thirds, n, group, LEN), jnp.float32),
            pltpu.VMEM((3, parts, group, SUB), jnp.float32),
        ],
        compiler_params=pltpu.CompilerParams(vmem_limit_bytes=48 * 1024 * 1024),
        cost_estimate=pl.CostEstimate(
            flops=12 * signal.size * LEN, bytes_accessed=8 * signal.size, transcendentals=0
        ),
    )(signal, taps, *tables)


def by_owner(value, n):
    rows = value.T.reshape(n, value.shape[1] // n, value.shape[0])
    return lax.all_to_all(rows, "ctx", split_axis=0, concat_axis=0, tiled=True)


def local(inputs, cotangent, filter_rows, skip_gain, band_blocks):
    n = lax.axis_size("ctx")
    block = inputs.shape[0]
    own = inputs.shape[1] // n
    start = lax.axis_index("ctx") * own
    gain = lax.dynamic_slice_in_dim(skip_gain, start, own)
    bands = lax.dynamic_slice_in_dim(band_blocks, start, own)
    tables = tuple(jnp.asarray(table) for table in transform_tables())

    taps = by_owner(filter_rows, n).transpose(1, 0, 2).reshape(own, -1)
    lag = jnp.arange(taps.shape[1], dtype=jnp.int32)[None, :]
    taps = jnp.where(lag < bands[:, None] * block, taps, 0.0)
    taps = taps + jnp.where(lag == 0, gain[:, None], 0.0)

    outputs = banded(by_owner(inputs, n), taps, tables, False)
    outputs = lax.all_to_all(outputs, "ctx", split_axis=0, concat_axis=0, tiled=True)
    outputs = outputs.reshape(n * own, block).T
    input_grad = banded(by_owner(cotangent, n), taps, tables, True)
    return outputs, input_grad


def solution(mesh):
    return jax.shard_map(
        local,
        mesh=mesh,
        in_specs=(P("ctx", "ch"), P("ctx", "ch"), P("ctx", "ch"), P("ch"), P("ch")),
        out_specs=(P("ctx", "ch"), P(("ch", "ctx"), None)),
        check_vma=False,
    )
```

```python
import functools

import jax
import jax.numpy as jnp
import numpy as np
from jax import lax
from jax.experimental import pallas as pl
from jax.experimental.pallas import tpu as pltpu
from jax.sharding import PartitionSpec as P

SUB = 256
LEN = 2 * SUB
JCHUNK = 4
OUTER = 4
BOTH = ("outer", "inner")


def stacked_halves(table):
    table = table.astype(np.float32)
    high = table.astype(jnp.bfloat16)
    low = (table - high.astype(np.float32)).astype(jnp.bfloat16)
    return np.concatenate([high, high, low], axis=0)


def transform_tables():
    time = np.arange(SUB)
    bins = np.arange(SUB)
    angle = 2.0 * np.pi * (time[:, None] * bins[None, :] % LEN) / LEN
    alternate = np.where(time % 2 == 0, 1.0, -1.0)
    real, imag = np.cos(angle), -np.sin(angle)
    imag[:, 0] = alternate
    forward = np.concatenate([real, imag], axis=1)
    back_real = 2.0 * np.cos(angle.T)
    back_real[0] = 1.0
    back_imag = -2.0 * np.sin(angle.T)
    back_imag[0] = alternate
    inverse = np.concatenate([back_real, back_imag], axis=0) / LEN
    return stacked_halves(forward), stacked_halves(inverse)


def precise_dot(value, table):
    high = value.astype(jnp.bfloat16)
    low = (value - high.astype(jnp.float32)).astype(jnp.bfloat16)
    return jnp.dot(
        jnp.concatenate([high, low, high], axis=1), table, preferred_element_type=jnp.float32
    )


def conv_kernel(adjoint, thirds, parts, *refs):
    *signals, h_ref, d_ref, i_ref, o_ref, w_ref, s_ref, t_ref = refs
    group = h_ref.shape[0]
    n = signals[-1].shape[0]
    total = sum(ref.shape[0] for ref in signals)
    halo = w_ref.shape[1] - n
    base = 0 if adjoint else halo
    lane = lax.broadcasted_iota(jnp.int32, (1, LEN), 1)
    sigma = jnp.where(lane % 2 == 0, 1.0, -1.0).astype(jnp.float32)
    first = lane[:, :SUB] == 0

    taps = jnp.concatenate([h_ref[:, p * SUB : (p + 1) * SUB] for p in range(parts)], axis=0)
    spec = precise_dot(taps, d_ref[...])
    real, imag = spec[:, :SUB], spec[:, SUB:]
    cross = jnp.where(first, 0.0, imag)
    t_ref[0] = real.reshape(parts, group, SUB)
    t_ref[1] = (-cross if adjoint else cross).reshape(parts, group, SUB)
    t_ref[2] = jnp.where(first, imag, real).reshape(parts, group, SUB)

    for t in range(thirds):
        rows = [ref[:, :, t * SUB : (t + 1) * SUB].reshape(-1, SUB) for ref in signals]
        spectra = precise_dot(jnp.concatenate(rows, axis=0), d_ref[...])
        s_ref[t] = spectra.reshape(total, group, LEN)

    if adjoint:
        w_ref[:, n : n + halo] = jnp.zeros((thirds, halo, group, LEN), jnp.float32)
    for t in range(thirds):
        if adjoint and t == thirds - 1:
            w_ref[t, n - 1] = s_ref[t, n - 1]
            w_ref[t, 0 : n - 1] = s_ref[t, 0 : n - 1] + sigma * s_ref[0, 1:n]
        elif adjoint:
            w_ref[t, 0:n] = s_ref[t] + sigma * s_ref[t + 1]
        elif t == 0:
            w_ref[0, 0] = s_ref[0, 0]
            w_ref[0, 1:total] = s_ref[0, 1:total] + sigma * s_ref[thirds - 1, 0 : total - 1]
        else:
            w_ref[t] = s_ref[t] + sigma * s_ref[t - 1]

    steps = n // JCHUNK

    def products(index, carry):
        rows = pl.ds(pl.multiple_of(index // steps * 8, 8), 8)
        start = index % steps * JCHUNK
        for t in range(thirds):
            acc_real = acc_imag = 0.0
            for p in range(parts):
                shift, third = divmod(t + p if adjoint else t - p, thirds)
                window = w_ref[third, pl.ds(start + base + shift, JCHUNK), rows, :]
                win_real, win_imag = window[..., :SUB], window[..., SUB:]
                tap_real, tap_cross, tap_last = (t_ref[i, p, rows, :] for i in range(3))
                acc_real += tap_real * win_real - tap_cross * win_imag
                acc_imag += tap_last * win_imag + tap_cross * win_real
            s_ref[t, pl.ds(start, JCHUNK), rows, :SUB] = acc_real
            s_ref[t, pl.ds(start, JCHUNK), rows, SUB:] = acc_imag
        return carry

    lax.fori_loop(0, steps * (group // 8), products, 0)

    for t in range(thirds):
        result = precise_dot(s_ref[t, 0:n].reshape(n * group, LEN), i_ref[...])
        result = result.reshape(n, group, SUB)
        if adjoint:
            for j in range(n):
                at = (j * thirds + t) * SUB
                o_ref[:, at : at + SUB] = result[j]
        else:
            o_ref[:, :, t * SUB : (t + 1) * SUB] = result


def banded(signals, taps, tables, adjoint):
    n, channels, block = signals[-1].shape
    thirds, parts = block // SUB, taps.shape[1] // SUB
    group = min(32, channels)
    halo = halo_blocks(block, taps)
    total = sum(signal.shape[0] for signal in signals)
    if adjoint:
        out_shape = (channels, n * block)
        out_spec = pl.BlockSpec((group, n * block), lambda g: (g, 0))
    else:
        out_shape = (n, channels, block)
        out_spec = pl.BlockSpec((n, group, block), lambda g: (0, g, 0))
    pieces = [
        pl.BlockSpec((signal.shape[0], group, block), lambda g: (0, g, 0)) for signal in signals
    ]
    whole = [pl.BlockSpec(table.shape, lambda g: (0, 0)) for table in tables]
    return pl.pallas_call(
        functools.partial(conv_kernel, adjoint, thirds, parts),
        out_shape=jax.ShapeDtypeStruct(out_shape, jnp.float32),
        grid=(channels // group,),
        in_specs=[*pieces, pl.BlockSpec((group, taps.shape[1]), lambda g: (g, 0)), *whole],
        out_specs=out_spec,
        scratch_shapes=[
            pltpu.VMEM((thirds, n + halo, group, LEN), jnp.float32),
            pltpu.VMEM((thirds, total, group, LEN), jnp.float32),
            pltpu.VMEM((3, parts, group, SUB), jnp.float32),
        ],
        compiler_params=pltpu.CompilerParams(vmem_limit_bytes=48 * 1024 * 1024),
        cost_estimate=pl.CostEstimate(
            flops=12 * n * channels * block * LEN,
            bytes_accessed=8 * n * channels * block,
            transcendentals=0,
        ),
    )(*signals, taps, *tables)


def halo_blocks(block, taps):
    thirds, parts = block // SUB, taps.shape[1] // SUB
    return (thirds + parts - 2) // thirds


def by_owner(value, n):
    rows = value.T.reshape(n, value.shape[1] // n, value.shape[0])
    return lax.all_to_all(rows, BOTH, split_axis=0, concat_axis=0, tiled=True)


def local(inputs, cotangent, filter_rows, skip_gain, band_blocks):
    outer, inner = lax.axis_size("outer"), lax.axis_size("inner")
    outer_at = lax.axis_index("outer")
    n = outer * inner
    block = inputs.shape[0]
    own = inputs.shape[1] // n
    start = (outer_at * inner + lax.axis_index("inner")) * own
    gain = lax.dynamic_slice_in_dim(skip_gain, start, own)
    bands = lax.dynamic_slice_in_dim(band_blocks, start, own)
    tables = tuple(jnp.asarray(table) for table in transform_tables())

    taps = by_owner(filter_rows, n).transpose(1, 0, 2).reshape(own, -1)
    lag = jnp.arange(taps.shape[1], dtype=jnp.int32)[None, :]
    taps = jnp.where(lag < bands[:, None] * block, taps, 0.0)
    taps = taps + jnp.where(lag == 0, gain[:, None], 0.0)
    column_taps = jnp.zeros((outer * own, taps.shape[1]), jnp.float32)
    for step in range(outer):
        piece = taps
        if step:
            ring = [(i, (i + step) % outer) for i in range(outer)]
            piece = lax.ppermute(taps, "outer", ring)
        row = (outer_at - step) % outer * own
        column_taps = lax.dynamic_update_slice(column_taps, piece, (row, 0))

    rows = inputs.T.reshape(outer, inner, own, block).transpose(1, 0, 2, 3)
    rows = rows.reshape(inner, outer * own, block)
    rows = lax.all_to_all(rows, "inner", split_axis=0, concat_axis=0, tiled=True)
    halo = halo_blocks(block, taps)
    before = lax.ppermute(rows[inner - halo :], "outer", [(i, i + 1) for i in range(outer - 1)])
    outputs = banded((before, rows), column_taps, tables, False)
    outputs = lax.all_to_all(outputs, "inner", split_axis=0, concat_axis=0, tiled=True)
    outputs = outputs.reshape(inner, outer, own, block).transpose(3, 1, 0, 2)
    outputs = outputs.reshape(block, n * own)

    input_grad = banded((by_owner(cotangent, n),), taps, tables, True)
    return outputs, input_grad


def solution(mesh):
    devices = mesh.devices
    devices = devices.reshape(OUTER, devices.shape[0] // OUTER, devices.shape[1])
    return jax.shard_map(
        local,
        mesh=jax.sharding.Mesh(devices, ("outer", "inner", "ch")),
        in_specs=(P(BOTH, "ch"), P(BOTH, "ch"), P(BOTH, "ch"), P("ch"), P("ch")),
        out_specs=(P(BOTH, "ch"), P(("ch", "outer", "inner"), None)),
        check_vma=False,
    )
```

```python
import functools

import jax
import jax.numpy as jnp
import numpy as np
from jax import lax
from jax.experimental import pallas as pl
from jax.experimental.pallas import tpu as pltpu
from jax.sharding import PartitionSpec as P

SUB = 256
LEN = 2 * SUB
JCHUNK = 4
OUTER = 4
BOTH = ("outer", "inner")


def stacked_halves(table):
    table = table.astype(np.float32)
    high = table.astype(jnp.bfloat16)
    low = (table - high.astype(np.float32)).astype(jnp.bfloat16)
    return np.concatenate([high, high, low], axis=0)


def transform_tables():
    time = np.arange(SUB)
    bins = np.arange(SUB)
    angle = 2.0 * np.pi * (time[:, None] * bins[None, :] % LEN) / LEN
    alternate = np.where(time % 2 == 0, 1.0, -1.0)
    real, imag = np.cos(angle), -np.sin(angle)
    imag[:, 0] = alternate
    forward = np.concatenate([real, imag], axis=1)
    back_real = 2.0 * np.cos(angle.T)
    back_real[0] = 1.0
    back_imag = -2.0 * np.sin(angle.T)
    back_imag[0] = alternate
    inverse = np.concatenate([back_real, back_imag], axis=0) / LEN
    return stacked_halves(forward), stacked_halves(inverse)


def precise_dot(value, table):
    high = value.astype(jnp.bfloat16)
    low = (value - high.astype(jnp.float32)).astype(jnp.bfloat16)
    return jnp.dot(
        jnp.concatenate([high, low, high], axis=1), table, preferred_element_type=jnp.float32
    )


def conv_kernel(adjoint, thirds, parts, *refs):
    *signals, h_ref, d_ref, i_ref, o_ref, w_ref, s_ref, t_ref = refs
    group = h_ref.shape[0]
    n = signals[-1].shape[0]
    total = sum(ref.shape[0] for ref in signals)
    halo = w_ref.shape[1] - n
    base = 0 if adjoint else halo
    lane = lax.broadcasted_iota(jnp.int32, (1, LEN), 1)
    sigma = jnp.where(lane % 2 == 0, 1.0, -1.0).astype(jnp.float32)
    first = lane[:, :SUB] == 0

    taps = jnp.concatenate([h_ref[:, p * SUB : (p + 1) * SUB] for p in range(parts)], axis=0)
    spec = precise_dot(taps, d_ref[...])
    real, imag = spec[:, :SUB], spec[:, SUB:]
    cross = jnp.where(first, 0.0, imag)
    t_ref[0] = real.reshape(parts, group, SUB)
    t_ref[1] = (-cross if adjoint else cross).reshape(parts, group, SUB)
    t_ref[2] = jnp.where(first, imag, real).reshape(parts, group, SUB)

    for t in range(thirds):
        rows = [ref[:, :, t * SUB : (t + 1) * SUB].reshape(-1, SUB) for ref in signals]
        spectra = precise_dot(jnp.concatenate(rows, axis=0), d_ref[...])
        s_ref[t] = spectra.reshape(total, group, LEN)

    if adjoint:
        w_ref[:, n : n + halo] = jnp.zeros((thirds, halo, group, LEN), jnp.float32)
    for t in range(thirds):
        if adjoint and t == thirds - 1:
            w_ref[t, n - 1] = s_ref[t, n - 1]
            w_ref[t, 0 : n - 1] = s_ref[t, 0 : n - 1] + sigma * s_ref[0, 1:n]
        elif adjoint:
            w_ref[t, 0:n] = s_ref[t] + sigma * s_ref[t + 1]
        elif t == 0:
            w_ref[0, 0] = s_ref[0, 0]
            w_ref[0, 1:total] = s_ref[0, 1:total] + sigma * s_ref[thirds - 1, 0 : total - 1]
        else:
            w_ref[t] = s_ref[t] + sigma * s_ref[t - 1]

    steps = n // JCHUNK

    def products(index, carry):
        rows = pl.ds(pl.multiple_of(index // steps * 8, 8), 8)
        start = index % steps * JCHUNK
        for t in range(thirds):
            acc_real = acc_imag = 0.0
            for p in range(parts):
                shift, third = divmod(t + p if adjoint else t - p, thirds)
                window = w_ref[third, pl.ds(start + base + shift, JCHUNK), rows, :]
                win_real, win_imag = window[..., :SUB], window[..., SUB:]
                tap_real, tap_cross, tap_last = (t_ref[i, p, rows, :] for i in range(3))
                acc_real += tap_real * win_real - tap_cross * win_imag
                acc_imag += tap_last * win_imag + tap_cross * win_real
            s_ref[t, pl.ds(start, JCHUNK), rows, :SUB] = acc_real
            s_ref[t, pl.ds(start, JCHUNK), rows, SUB:] = acc_imag
        return carry

    lax.fori_loop(0, steps * (group // 8), products, 0)

    for t in range(thirds):
        result = precise_dot(s_ref[t, 0:n].reshape(n * group, LEN), i_ref[...])
        result = result.reshape(n, group, SUB)
        if adjoint:
            for j in range(n):
                at = (j * thirds + t) * SUB
                o_ref[:, at : at + SUB] = result[j]
        else:
            o_ref[:, :, t * SUB : (t + 1) * SUB] = result


def banded(signals, taps, tables, adjoint):
    n, channels, block = signals[-1].shape
    thirds, parts = block // SUB, taps.shape[1] // SUB
    group = min(32, channels)
    halo = halo_blocks(block, taps)
    total = sum(signal.shape[0] for signal in signals)
    if adjoint:
        out_shape = (channels, n * block)
        out_spec = pl.BlockSpec((group, n * block), lambda g: (g, 0))
    else:
        out_shape = (n, channels, block)
        out_spec = pl.BlockSpec((n, group, block), lambda g: (0, g, 0))
    pieces = [
        pl.BlockSpec((signal.shape[0], group, block), lambda g: (0, g, 0)) for signal in signals
    ]
    whole = [pl.BlockSpec(table.shape, lambda g: (0, 0)) for table in tables]
    return pl.pallas_call(
        functools.partial(conv_kernel, adjoint, thirds, parts),
        out_shape=jax.ShapeDtypeStruct(out_shape, jnp.float32),
        grid=(channels // group,),
        in_specs=[*pieces, pl.BlockSpec((group, taps.shape[1]), lambda g: (g, 0)), *whole],
        out_specs=out_spec,
        scratch_shapes=[
            pltpu.VMEM((thirds, n + halo, group, LEN), jnp.float32),
            pltpu.VMEM((thirds, total, group, LEN), jnp.float32),
            pltpu.VMEM((3, parts, group, SUB), jnp.float32),
        ],
        compiler_params=pltpu.CompilerParams(vmem_limit_bytes=48 * 1024 * 1024),
        cost_estimate=pl.CostEstimate(
            flops=12 * n * channels * block * LEN,
            bytes_accessed=8 * n * channels * block,
            transcendentals=0,
        ),
    )(*signals, taps, *tables)


def halo_blocks(block, taps):
    thirds, parts = block // SUB, taps.shape[1] // SUB
    return (thirds + parts - 2) // thirds


def swapped(value, axis):
    return lax.all_to_all(value, axis, split_axis=0, concat_axis=0, tiled=True)


def local(inputs, cotangent, filter_rows, skip_gain, band_blocks):
    outer, inner = lax.axis_size("outer"), lax.axis_size("inner")
    outer_at, inner_at = lax.axis_index("outer"), lax.axis_index("inner")
    block, channels = inputs.shape
    own = channels // (outer * inner)
    column = outer * own
    tap_rows = filter_rows.shape[0]
    tables = tuple(jnp.asarray(table) for table in transform_tables())

    tap_grid = jnp.zeros((outer, tap_rows, channels), jnp.float32)
    for step in range(outer):
        piece = filter_rows
        if step:
            ring = [(i, (i + step) % outer) for i in range(outer)]
            piece = lax.ppermute(piece, "outer", ring)
        at = (outer_at - step) % outer
        tap_grid = lax.dynamic_update_slice(tap_grid, piece[None], (at, 0, 0))

    rows = inputs.T.reshape(outer, inner, own, block).transpose(1, 0, 2, 3)
    rows = swapped(rows.reshape(inner, column, block), "inner")
    rows, tap_grid = lax.optimization_barrier((rows, tap_grid))
    halo = (block // SUB + outer * inner * tap_rows // SUB - 2) // (block // SUB)
    before = lax.ppermute(rows[inner - halo :], "outer", [(i, i + 1) for i in range(outer - 1)])

    taps = tap_grid.transpose(2, 0, 1).reshape(outer, inner, own, outer * tap_rows)
    taps = taps.transpose(1, 0, 2, 3).reshape(inner, column, outer * tap_rows)
    taps = swapped(taps, "inner")
    grad_rows = cotangent.T.reshape(outer * inner, own, block)
    taps, before, grad_rows = lax.optimization_barrier((taps, before, grad_rows))
    grad_rows = swapped(grad_rows, BOTH)
    taps = taps.reshape(inner, column, outer, tap_rows).transpose(1, 2, 0, 3).reshape(column, -1)
    of_column = lambda value: lax.dynamic_slice_in_dim(
        value.reshape(outer, inner, own), inner_at, 1, axis=1
    ).reshape(column, 1)
    lag = jnp.arange(taps.shape[1], dtype=jnp.int32)[None, :]
    taps = jnp.where(lag < of_column(band_blocks) * block, taps, 0.0)
    taps = taps + jnp.where(lag == 0, of_column(skip_gain), 0.0)

    forward = banded((before, rows), taps, tables, False)
    outputs = jnp.zeros((inner, column, block), jnp.float32)
    for step in range(inner):
        piece = lax.dynamic_slice_in_dim(forward, (inner_at + step) % inner, 1, axis=0)
        if step:
            ring = [(i, (i + step) % inner) for i in range(inner)]
            piece = lax.ppermute(piece, "inner", ring)
        outputs = lax.dynamic_update_slice(outputs, piece, ((inner_at - step) % inner, 0, 0))
    outputs = outputs.reshape(inner, outer, own, block).transpose(3, 1, 0, 2)
    outputs = outputs.reshape(block, channels)

    own_taps = lax.dynamic_slice_in_dim(taps, outer_at * own, own)
    input_grad = banded((grad_rows,), own_taps, tables, True)
    return outputs, input_grad


def solution(mesh):
    devices = mesh.devices
    devices = devices.reshape(OUTER, devices.shape[0] // OUTER, devices.shape[1])
    return jax.shard_map(
        local,
        mesh=jax.sharding.Mesh(devices, ("outer", "inner", "ch")),
        in_specs=(P(BOTH, "ch"), P(BOTH, "ch"), P(BOTH, "ch"), P("ch"), P("ch")),
        out_specs=(P(BOTH, "ch"), P(("ch", "outer", "inner"), None)),
        check_vma=False,
    )
```
